32 devices in a mesh: row: 8 (over z, core), col: 4 (over y, x).
Axes of the slice: x: 2, y: 2, z: 4, core: 2. Of those that a mesh axis runs over, the one named last changes fastest.
Arguments:
- similarity: bfloat16 [2048, 2048], P('row', 'col')
- in_mask: int32 [8, 8], P('row', 'col'), may hold values from 0 to 1, as said below
- out_mask: int32 [8, 8], P('row', 'col'), may hold values from 0 to 1, as said below
Outputs:
- stochastic: float32 [2048, 2048], P('row', 'col')
The draws below stay inside these ranges and needn't reach their ends.
Inputs may be any that keep to these rules, and one draw needn't show every extreme that they name: in_mask is symmetric, similarity is symmetric and nonnegative with positive diagonal entries, and every diagonal block is present. `out_mask`: every diagonal block is kept.
All inputs are finite; a program needn't handle non-finite values.
Results may differ from the reference program's by a relative error of at most 0.0003.
Values may be sent and summed in bfloat16 or wider, within the bound.
No kernel may reach another device: no remote copies, remote signals or barrier semaphores. Data moves between devices by JAX's collectives and lax.ppermute only.
A program may use at most 64 MiB of HBM per device.

```python
import jax
import jax.numpy as jnp
from jax import lax

BS = 256
NB = 8
N = 2048


def draw_similarity(key, part):
    base = jax.random.fold_in(key, 3)
    first = jax.random.fold_in(base, 1)
    second = jax.random.fold_in(base, 2)
    third = jax.random.fold_in(base, 4)
    uniform_part = jax.random.uniform(first, (N, N), jnp.float32, 0.0, 1.0)
    kept = jax.random.randint(third, (N, N), 0, 4) < 3
    values = -jnp.log1p(-uniform_part)
    scales = jnp.exp(jax.random.uniform(second, (N,), jnp.float32, 0.0, 1.15))
    raw = jnp.where(kept, values, jnp.float32(0.0))
    rows = jnp.arange(N, dtype=jnp.int32)[:, None]
    cols = jnp.arange(N, dtype=jnp.int32)[None, :]
    sym = jnp.where(rows <= cols, raw, raw.T)
    sym = jnp.where(rows == cols, 1.0 + sym, sym)
    return (scales[:, None] * scales[None, :] * sym).astype(jnp.bfloat16)


def draw_in_mask(key, part):
    bits = jax.random.randint(jax.random.fold_in(key, 1), (NB, NB), 0, 2)
    rows = lax_rows(NB)
    cols = rows.T
    sym = jnp.where(rows <= cols, bits, bits.T)
    return jnp.where(rows == cols, 1, sym).astype(jnp.int32)


def draw_out_mask(key, part):
    bits = jax.random.randint(jax.random.fold_in(key, 2), (NB, NB), 0, 2)
    rows = lax_rows(NB)
    return jnp.where(rows == rows.T, 1, bits).astype(jnp.int32)


def lax_rows(count):
    return jnp.broadcast_to(jnp.arange(count, dtype=jnp.int32)[:, None], (count, count))


def setup_inputs(seed: int = 0) -> dict:
    arg_keys = jax.random.split(jax.random.key(seed), 4)
    similarity = draw_similarity(jax.random.fold_in(arg_keys[3], 71), 0)
    in_mask = draw_in_mask(jax.random.fold_in(arg_keys[3], 71), 0)
    out_mask = draw_out_mask(jax.random.fold_in(arg_keys[3], 71), 0)
    return {"similarity": similarity, "in_mask": in_mask, "out_mask": out_mask}


def reference(similarity, in_mask, out_mask):
    live = in_mask.astype(jnp.bfloat16)[:, None, :, None]
    sparse = (similarity.reshape(NB, BS, NB, BS) * live).reshape(N, N)
    wide = sparse.astype(jnp.float32)
    product = jnp.dot(wide, wide, precision=lax.Precision.HIGHEST, preferred_element_type=jnp.float32)
    keep = out_mask.astype(jnp.float32)[:, None, :, None]
    kept = (product.reshape(NB, BS, NB, BS) * keep).reshape(N, N)
    inflated = kept * kept
    column_sums = jnp.sum(inflated, axis=0)
    return inflated * (jnp.float32(N) / column_sums)[None, :]
```

```python
import functools

import jax
import jax.numpy as jnp
from jax import lax
from jax.experimental import pallas as pl
from jax.experimental.pallas import tpu as pltpu
from jax.sharding import PartitionSpec as P

BS = 256


def swap(value, axis, size, mask):
    return lax.ppermute(value, axis, [(i, i ^ mask) for i in range(size)])


def early_kernel(n_col, n_z, last, place, *refs):
    panels = refs[:n_col]
    mine = refs[n_col : n_col + n_z - 1]
    theirs = refs[n_col + n_z - 1 : n_col + 2 * (n_z - 1)]
    acc_ref, late_ref, slots = refs[n_col + 2 * (n_z - 1) :]
    z, core, col = place[0], place[1], place[2]
    for j in range(n_col):
        slots[col ^ j] = panels[j][...]
    here = pl.ds(pl.multiple_of(core * BS, BS), BS)
    there = pl.ds(pl.multiple_of((1 - core) * BS, BS), BS)
    acc = None
    planes = [m for m in range(n_z) if m != last]
    for m, own, other in zip(planes, mine, theirs):
        panel = slots.at[z ^ m]
        term = jnp.dot(panel[:, here], own[...], preferred_element_type=jnp.float32)
        term += jnp.dot(panel[:, there], other[...], preferred_element_type=jnp.float32)
        acc = term if acc is None else acc + term
    acc_ref[...] = acc
    late_ref[...] = slots[z ^ last]


def late_kernel(place, keep, acc_ref, panel, own, other, out_ref, sums_ref):
    core = place[1]
    here = pl.ds(pl.multiple_of(core * BS, BS), BS)
    there = pl.ds(pl.multiple_of((1 - core) * BS, BS), BS)
    product = acc_ref[...]
    product += jnp.dot(panel[:, here], own[...], preferred_element_type=jnp.float32)
    product += jnp.dot(panel[:, there], other[...], preferred_element_type=jnp.float32)
    for b in range(product.shape[1] // BS):
        kept = jnp.where(keep[0, b] != 0, product[:, b * BS : (b + 1) * BS], 0.0)
        inflated = kept * kept
        out_ref[:, b * BS : (b + 1) * BS] = inflated
        sums_ref[:, b * BS : (b + 1) * BS] = jnp.sum(inflated, axis=0, keepdims=True)


def on_device(n_row, n_col, similarity, in_mask, out_mask):
    rows_loc, cols_loc = similarity.shape
    rblocks, cblocks = in_mask.shape
    n_z = n_row // 2
    live = in_mask.astype(jnp.bfloat16)[:, None, :, None]
    sparse = (similarity.reshape(rblocks, BS, cblocks, BS) * live).reshape(rows_loc, cols_loc)

    row = lax.axis_index("row")
    place = jnp.stack([row // 2, row % 2, lax.axis_index("col")]).astype(jnp.int32)

    mine = {m: swap(sparse, "row", n_row, 2 * m) for m in range(n_z - 1, 0, -1)}
    panels = [sparse] + [swap(sparse, "col", n_col, j) for j in range(1, n_col)]
    mine[0] = sparse
    theirs = {m: swap(mine[m], "row", n_row, 1) for m in range(n_z)}

    last = max(n_z // 2, 1)
    planes = [m for m in range(n_z) if m != last]
    smem = pl.BlockSpec(memory_space=pltpu.SMEM)
    vmem = pl.BlockSpec(memory_space=pltpu.VMEM)
    operands = panels + [mine[m] for m in planes] + [theirs[m] for m in planes]
    acc, late_panel = pl.pallas_call(
        functools.partial(early_kernel, n_col, n_z, last),
        out_shape=(
            jax.ShapeDtypeStruct((rows_loc, cols_loc), jnp.float32),
            jax.ShapeDtypeStruct((rows_loc, cols_loc), jnp.bfloat16),
        ),
        in_specs=[smem] + [vmem] * len(operands),
        out_specs=(vmem, vmem),
        scratch_shapes=[pltpu.VMEM((n_col, rows_loc, cols_loc), jnp.bfloat16)],
    )(place, *operands)
    inflated, sums = pl.pallas_call(
        late_kernel,
        out_shape=(
            jax.ShapeDtypeStruct((rows_loc, cols_loc), jnp.float32),
            jax.ShapeDtypeStruct((1, cols_loc), jnp.float32),
        ),
        in_specs=[smem, smem] + [vmem] * 4,
        out_specs=(vmem, vmem),
    )(place, out_mask, acc, late_panel, mine[last], theirs[last])

    step = 1
    while step < n_row:
        sums = sums + swap(sums, "row", n_row, step)
        step *= 2
    total = jnp.float32(rows_loc * n_row)
    return inflated * (total / sums)


def solution(mesh):
    in_specs = (P("row", "col"), P("row", "col"), P("row", "col"))
    out_specs = P("row", "col")
    body = functools.partial(on_device, mesh.shape["row"], mesh.shape["col"])
    return jax.shard_map(
        body, mesh=mesh, in_specs=in_specs, out_specs=out_specs, check_vma=False
    )
```

```python
import functools

import jax
import jax.numpy as jnp
from jax import lax
from jax.experimental import pallas as pl
from jax.experimental.pallas import tpu as pltpu
from jax.sharding import PartitionSpec as P

BS = 256


def swap(value, axis, size, mask):
    return lax.ppermute(value, axis, [(i, i ^ mask) for i in range(size)])


def along_z(value, pairs):
    return lax.ppermute(value, "row", [(2 * s + k, 2 * t + k) for s, t in pairs for k in (0, 1)])


def resident(value):
    return pltpu.with_memory_space_constraint(value, pltpu.VMEM)


def term(panel, core, own, other):
    here = pl.ds(pl.multiple_of(core * BS, BS), BS)
    there = pl.ds(pl.multiple_of((1 - core) * BS, BS), BS)
    return jnp.dot(
        panel[:, here], own[...], preferred_element_type=jnp.float32
    ) + jnp.dot(panel[:, there], other[...], preferred_element_type=jnp.float32)


def early_kernel(n_col, planes, last, place, *refs):
    panels = refs[:n_col]
    mine = refs[n_col : n_col + len(planes)]
    theirs = refs[n_col + len(planes) : n_col + 2 * len(planes)]
    acc_ref, late_ref, slots = refs[n_col + 2 * len(planes) :]
    z, core, col = place[0], place[1], place[2]
    for j in range(n_col):
        slots[col ^ j] = panels[j][...]
    acc = None
    for m, own, other in zip(planes, mine, theirs):
        part = term(slots.at[z ^ m], core, own, other)
        acc = part if acc is None else acc + part
    acc_ref[...] = acc
    late_ref[...] = slots[z ^ last]


def late_kernel(place, keep, acc_ref, panel, own, other, out_ref, sums_ref):
    product = acc_ref[...] + term(panel, place[1], own, other)
    for b in range(product.shape[1] // BS):
        kept = jnp.where(keep[0, b] != 0, product[:, b * BS : (b + 1) * BS], 0.0)
        inflated = kept * kept
        out_ref[:, b * BS : (b + 1) * BS] = inflated
        sums_ref[:, b * BS : (b + 1) * BS] = jnp.sum(inflated, axis=0, keepdims=True)


def gather(sparse, n_row, n_col):
    n_z = n_row // 2
    ends = n_z == 4
    panels = {1 << i: swap(sparse, "col", n_col, 1 << i) for i in range(n_col.bit_length() - 1)}
    if ends:
        blocks = {m: along_z(sparse, [(i, i ^ m) for i in range(4)]) for m in (1, 2)}
    else:
        blocks = {m: swap(sparse, "row", n_row, 2 * m) for m in range(1, n_z)}
    other = swap(sparse, "row", n_row, 1)
    names = [(blocks, m) for m in sorted(blocks, reverse=True)]
    names += [(panels, j) for j in sorted(panels)]
    *moved, other, source = lax.optimization_barrier([d[k] for d, k in names] + [other, sparse])
    for (d, k), value in zip(names, moved):
        d[k] = value
    if ends:
        middle = along_z(source, [(1, 2), (2, 1)])
        pairs = [(1, blocks[1]), (2, blocks[2]), (3, middle)]
        pairs.append((3, along_z(blocks[2], [(1, 0), (2, 3)])))
    else:
        pairs = list(blocks.items())
    panels[0] = sparse
    for j in range(n_col):
        if j not in panels:
            low = j & -j
            panels[j] = swap(panels[j ^ low], "col", n_col, low)
    theirs = [other] + [swap(block, "row", n_row, 1) for _, block in pairs]
    return [panels[j] for j in range(n_col)], [(0, sparse)] + pairs, theirs


def on_device(n_row, n_col, similarity, in_mask, out_mask):
    rows_loc, cols_loc = similarity.shape
    rblocks, cblocks = in_mask.shape
    live = in_mask.astype(jnp.bfloat16)[:, None, :, None]
    sparse = (similarity.reshape(rblocks, BS, cblocks, BS) * live).reshape(rows_loc, cols_loc)

    row = lax.axis_index("row")
    place = jnp.stack([row // 2, row % 2, lax.axis_index("col")]).astype(jnp.int32)
    panels, mine, theirs = gather(sparse, n_row, n_col)
    last, late = mine.pop()
    other = theirs.pop()

    smem = pl.BlockSpec(memory_space=pltpu.SMEM)
    vmem = pl.BlockSpec(memory_space=pltpu.VMEM)
    size = 2 * rows_loc * cols_loc
    operands = panels + [block for _, block in mine] + theirs
    acc, late_panel = pl.pallas_call(
        functools.partial(early_kernel, n_col, [m for m, _ in mine], last),
        out_shape=(
            pltpu.VMEM((rows_loc, cols_loc), jnp.float32),
            pltpu.VMEM((rows_loc, cols_loc), jnp.bfloat16),
        ),
        in_specs=[smem] + [vmem] * len(operands),
        out_specs=(vmem, vmem),
        scratch_shapes=[pltpu.VMEM((n_col, rows_loc, cols_loc), jnp.bfloat16)],
        compiler_params=pltpu.CompilerParams(vmem_limit_bytes=(n_col + 8) * size),
    )(place, *map(resident, operands))
    inflated, sums = pl.pallas_call(
        late_kernel,
        out_shape=(
            pltpu.VMEM((rows_loc, cols_loc), jnp.float32),
            pltpu.VMEM((1, cols_loc), jnp.float32),
        ),
        in_specs=[smem, smem] + [vmem] * 4,
        out_specs=(vmem, vmem),
        compiler_params=pltpu.CompilerParams(vmem_limit_bytes=8 * size),
    )(place, out_mask, acc, late_panel, resident(late), resident(other))

    step = 1
    while step < n_row:
        sums = sums + swap(sums, "row", n_row, step)
        step *= 2
    total = jnp.float32(rows_loc * n_row)
    return inflated * (total / sums)


def solution(mesh):
    in_specs = (P("row", "col"), P("row", "col"), P("row", "col"))
    out_specs = P("row", "col")
    body = functools.partial(on_device, mesh.shape["row"], mesh.shape["col"])
    return jax.shard_map(
        body, mesh=mesh, in_specs=in_specs, out_specs=out_specs, check_vma=False
    )
```

```python
import functools

import jax
import jax.numpy as jnp
from jax import lax
from jax.experimental import pallas as pl
from jax.experimental.pallas import tpu as pltpu
from jax.sharding import PartitionSpec as P

BS = 256
HALF = BS // 2
SMEM = pl.BlockSpec(memory_space=pltpu.SMEM)
VMEM = pl.BlockSpec(memory_space=pltpu.VMEM)


def swap(value, axis, size, mask):
    return lax.ppermute(value, axis, [(i, i ^ mask) for i in range(size)])


def along_z(value, pairs):
    return lax.ppermute(value, "row", [(2 * s + k, 2 * t + k) for s, t in pairs for k in (0, 1)])


def after(value, *others):
    return lax.optimization_barrier((value, *others))[0]


def resident(value):
    return pltpu.with_memory_space_constraint(value, pltpu.VMEM)


def mask_kernel(live_hbm, keep_hbm, similarity_hbm, *rest):
    *blocks, keep, live, similarity, sems = rest
    copies = [
        pltpu.make_async_copy(similarity_hbm, similarity, sems.at[0]),
        pltpu.make_async_copy(live_hbm, live, sems.at[1]),
        pltpu.make_async_copy(keep_hbm, keep, sems.at[2]),
    ]
    for copy in copies:
        copy.start()
    for copy in copies[::-1]:
        copy.wait()
    for b in range(similarity.shape[1] // BS):
        cols = slice(b * BS, (b + 1) * BS)
        kept = similarity[:, cols]
        kept = jnp.where(live[0, b] != 0, kept, jnp.zeros_like(kept))
        for (first, count), block in zip(split(len(blocks)), blocks):
            block[:, cols] = kept[first : first + count]


def split(blocks):
    return [(0, BS), (0, HALF), (HALF, HALF)][:blocks]


def masked(similarity, in_mask, out_mask, halves):
    cols = similarity.shape[1]
    shapes = [pltpu.VMEM((n, cols), jnp.bfloat16) for _, n in split(3 if halves else 1)]
    hbm = pl.BlockSpec(memory_space=pltpu.HBM)
    operands = [in_mask, out_mask, similarity]
    return pl.pallas_call(
        mask_kernel,
        out_shape=shapes + [pltpu.SMEM(out_mask.shape, jnp.int32)],
        in_specs=[hbm] * 3,
        out_specs=[VMEM] * len(shapes) + [SMEM],
        scratch_shapes=[
            pltpu.SMEM(in_mask.shape, jnp.int32),
            pltpu.VMEM(similarity.shape, jnp.bfloat16),
            pltpu.SemaphoreType.DMA((3,)),
        ],
        compiler_params=pltpu.CompilerParams(vmem_limit_bytes=16 * BS * cols),
    )(*[pltpu.with_memory_space_constraint(value, pltpu.HBM) for value in operands])


def term(panel, core, first, own, other):
    rows = own.shape[0]
    here = pl.ds(pl.multiple_of(core * BS + first, HALF), rows)
    there = pl.ds(pl.multiple_of((1 - core) * BS + first, HALF), rows)
    return jnp.dot(
        panel[:, here], own[...], preferred_element_type=jnp.float32
    ) + jnp.dot(panel[:, there], other[...], preferred_element_type=jnp.float32)


def early_kernel(n_col, pieces, last, *refs):
    panels = refs[:n_col]
    mine = refs[n_col : n_col + len(pieces)]
    theirs = refs[n_col + len(pieces) : n_col + 2 * len(pieces)]
    acc_ref, late_ref, slots = refs[n_col + 2 * len(pieces) :]
    row, col = lax.axis_index("row"), lax.axis_index("col")
    z, core = row // 2, row % 2
    for j in range(n_col):
        slots[col ^ j] = panels[j][...]
    acc = None
    for (m, first), own, other in zip(pieces, mine, theirs):
        part = term(slots.at[z ^ m], core, first, own, other)
        acc = part if acc is None else acc + part
    acc_ref[...] = acc
    late_ref[...] = slots[z ^ last]


def late_kernel(first, keep, acc_ref, panel, own, other, out_ref, sums_ref):
    core = lax.axis_index("row") % 2
    product = acc_ref[...] + term(panel, core, first, own, other)
    for b in range(product.shape[1] // BS):
        cols = slice(b * BS, (b + 1) * BS)
        kept = jnp.where(keep[0, b] != 0, product[:, cols], 0.0)
        inflated = kept * kept
        out_ref[:, cols] = inflated
        sums_ref[:, cols] = jnp.sum(inflated, axis=0, keepdims=True)


def gather_line(sparse, halves, n_row, n_col):
    two = [(i, i ^ 2) for i in range(4)]
    out = [(1, 0), (2, 3)]

    def share(value, *others):
        return swap(after(value, *others) if others else value, "row", n_row, 1)

    top = along_z(halves[0], two)
    own = share(sparse, top)
    x = swap(sparse, "col", n_col, 1)
    y = swap(sparse, "col", n_col, 2)
    one = along_z(sparse, [(i, i ^ 1) for i in range(4)])
    bottom = along_z(halves[1], two)
    far_top = along_z(after(top, x), out)
    middle = along_z(after(sparse, top, x, y), [(1, 2), (2, 1)])
    xy = swap(after(y, top), "col", n_col, 1)
    ones = share(one)
    far_bottom = along_z(bottom, out)
    tops = share(top, bottom, far_top)
    bottoms = share(bottom, far_top, xy)
    middles = share(middle)
    far_tops = share(far_top)
    far_bottoms = share(far_bottom, y)
    return [sparse, x, y, xy], [
        (2, 0, top, tops),
        (3, 0, middle, middles),
        (1, 0, one, ones),
        (3, 0, far_top, far_tops),
        (0, 0, sparse, own),
        (2, HALF, bottom, bottoms),
        (3, HALF, far_bottom, far_bottoms),
    ]


def gather(sparse, n_row, n_col):
    panels = [sparse]
    while len(panels) < n_col:
        panels += [swap(panel, "col", n_col, len(panels)) for panel in panels]
    blocks = [sparse] + [swap(sparse, "row", n_row, 2 * m) for m in range(1, n_row // 2)]
    return panels, [(m, 0, own, swap(own, "row", n_row, 1)) for m, own in enumerate(blocks)]


def on_device(n_row, n_col, similarity, in_mask, out_mask):
    rows_loc, cols_loc = similarity.shape
    line = (n_row, n_col) == (8, 4)
    sparse, *halves, keep = masked(similarity, in_mask, out_mask, line)
    if line:
        panels, pieces = gather_line(sparse, halves, n_row, n_col)
    else:
        panels, pieces = gather(sparse, n_row, n_col)
    where = [(m, first) for m, first, _, _ in pieces]
    mine = [own for _, _, own, _ in pieces]
    theirs = [other for _, _, _, other in pieces]

    size = 2 * rows_loc * cols_loc
    operands = panels + mine[:-1] + theirs[:-1]
    acc, late_panel = pl.pallas_call(
        functools.partial(early_kernel, n_col, where[:-1], where[-1][0]),
        out_shape=(
            pltpu.VMEM((rows_loc, cols_loc), jnp.float32),
            pltpu.VMEM((rows_loc, cols_loc), jnp.bfloat16),
        ),
        in_specs=[VMEM] * len(operands),
        out_specs=(VMEM, VMEM),
        scratch_shapes=[pltpu.VMEM((n_col, rows_loc, cols_loc), jnp.bfloat16)],
        compiler_params=pltpu.CompilerParams(vmem_limit_bytes=(n_col + 8) * size),
    )(*map(resident, operands))
    inflated, sums = pl.pallas_call(
        functools.partial(late_kernel, where[-1][1]),
        out_shape=(
            pltpu.VMEM((rows_loc, cols_loc), jnp.float32),
            pltpu.VMEM((1, cols_loc), jnp.float32),
        ),
        in_specs=[SMEM] + [VMEM] * 4,
        out_specs=(VMEM, VMEM),
        compiler_params=pltpu.CompilerParams(vmem_limit_bytes=8 * size),
    )(keep, acc, late_panel, resident(mine[-1]), resident(theirs[-1]))

    step = 1
    while step < n_row:
        sums = sums + swap(sums, "row", n_row, step)
        step *= 2
    total = jnp.float32(rows_loc * n_row)
    return inflated * (total / sums)


def solution(mesh):
    in_specs = (P("row", "col"), P("row", "col"), P("row", "col"))
    out_specs = P("row", "col")
    body = functools.partial(on_device, mesh.shape["row"], mesh.shape["col"])
    return jax.shard_map(
        body, mesh=mesh, in_specs=in_specs, out_specs=out_specs, check_vma=False
    )
```

```python
import functools

import jax
import jax.numpy as jnp
from jax import lax
from jax.experimental import pallas as pl
from jax.experimental.pallas import tpu as pltpu
from jax.sharding import PartitionSpec as P

BS = 256
HALF = BS // 2
SMEM = pl.BlockSpec(memory_space=pltpu.SMEM)
VMEM = pl.BlockSpec(memory_space=pltpu.VMEM)


def swap(value, axis, size, mask):
    return lax.ppermute(value, axis, [(i, i ^ mask) for i in range(size)])


def along_z(value, pairs):
    return lax.ppermute(value, "row", [(2 * s + k, 2 * t + k) for s, t in pairs for k in (0, 1)])


def after(value, *others):
    return lax.optimization_barrier((value, *others))[0]


def resident(value):
    return pltpu.with_memory_space_constraint(value, pltpu.VMEM)


def mask_kernel(live_hbm, keep_hbm, similarity_hbm, *rest):
    *blocks, keep, live, similarity, sems = rest
    copies = [
        pltpu.make_async_copy(similarity_hbm, similarity, sems.at[0]),
        pltpu.make_async_copy(live_hbm, live, sems.at[1]),
        pltpu.make_async_copy(keep_hbm, keep, sems.at[2]),
    ]
    for copy in copies:
        copy.start()
    for copy in copies[::-1]:
        copy.wait()
    for b in range(similarity.shape[1] // BS):
        cols = slice(b * BS, (b + 1) * BS)
        kept = similarity[:, cols]
        kept = jnp.where(live[0, b] != 0, kept, jnp.zeros_like(kept))
        for (first, count), block in zip(split(len(blocks)), blocks):
            block[:, cols] = kept[first : first + count]


def split(blocks):
    return [(0, BS), (0, HALF), (HALF, HALF)][:blocks]


def masked(similarity, in_mask, out_mask, halves):
    cols = similarity.shape[1]
    shapes = [pltpu.VMEM((n, cols), jnp.bfloat16) for _, n in split(3 if halves else 1)]
    hbm = pl.BlockSpec(memory_space=pltpu.HBM)
    operands = [in_mask, out_mask, similarity]
    return pl.pallas_call(
        mask_kernel,
        out_shape=shapes + [pltpu.SMEM(out_mask.shape, jnp.int32)],
        in_specs=[hbm] * 3,
        out_specs=[VMEM] * len(shapes) + [SMEM],
        scratch_shapes=[
            pltpu.SMEM(in_mask.shape, jnp.int32),
            pltpu.VMEM(similarity.shape, jnp.bfloat16),
            pltpu.SemaphoreType.DMA((3,)),
        ],
        compiler_params=pltpu.CompilerParams(vmem_limit_bytes=16 * BS * cols),
    )(*[pltpu.with_memory_space_constraint(value, pltpu.HBM) for value in operands])


def join_kernel(top, bottom, out):
    out[:HALF] = top[...]
    out[HALF:] = bottom[...]


def pick_kernel(top, bottom, middle, out):
    z = lax.axis_index("row") // 2
    at_end = jnp.logical_or(z == 0, z == 3)

    @pl.when(at_end)
    def _():
        join_kernel(top, bottom, out)

    @pl.when(jnp.logical_not(at_end))
    def _():
        out[...] = middle[...]


def joined(kernel, *blocks):
    return pl.pallas_call(
        kernel,
        out_shape=pltpu.VMEM((BS, blocks[0].shape[1]), jnp.bfloat16),
        in_specs=[VMEM] * len(blocks),
        out_specs=VMEM,
        compiler_params=pltpu.CompilerParams(vmem_limit_bytes=16 * BS * BS),
    )(*map(resident, blocks))


def term(panel, core, own, other):
    here = pl.ds(pl.multiple_of(core * BS, BS), BS)
    there = pl.ds(pl.multiple_of((1 - core) * BS, BS), BS)
    return jnp.dot(
        panel[:, here], own[...], preferred_element_type=jnp.float32
    ) + jnp.dot(panel[:, there], other[...], preferred_element_type=jnp.float32)


def early_kernel(n_col, pieces, last, *refs):
    panels = refs[:n_col]
    mine = refs[n_col : n_col + len(pieces)]
    theirs = refs[n_col + len(pieces) : n_col + 2 * len(pieces)]
    acc_ref, late_ref, slots = refs[n_col + 2 * len(pieces) :]
    row, col = lax.axis_index("row"), lax.axis_index("col")
    z, core = row // 2, row % 2
    for j in range(n_col):
        slots[col ^ j] = panels[j][...]
    acc = None
    for m, own, other in zip(pieces, mine, theirs):
        part = term(slots.at[z ^ m], core, own, other)
        acc = part if acc is None else acc + part
    acc_ref[...] = acc
    late_ref[...] = slots[z ^ last]


def late_kernel(keep, acc_ref, panel, own, other, out_ref, sums_ref):
    core = lax.axis_index("row") % 2
    product = acc_ref[...] + term(panel, core, own, other)
    for b in range(product.shape[1] // BS):
        cols = slice(b * BS, (b + 1) * BS)
        kept = jnp.where(keep[0, b] != 0, product[:, cols], 0.0)
        inflated = kept * kept
        out_ref[:, cols] = inflated
        sums_ref[:, cols] = jnp.sum(inflated, axis=0, keepdims=True)


def gather_line(sparse, halves, n_row, n_col):
    two = [(i, i ^ 2) for i in range(4)]
    out = [(1, 0), (2, 3)]

    def share(value, *others):
        return swap(after(value, *others) if others else value, "row", n_row, 1)

    top = along_z(halves[0], two)
    x = swap(sparse, "col", n_col, 1)
    y = swap(sparse, "col", n_col, 2)
    one = along_z(sparse, [(i, i ^ 1) for i in range(4)])
    bottom = along_z(halves[1], two)
    end_top = along_z(top, out)
    middle = along_z(after(sparse, top, x), [(1, 2), (2, 1)])
    xy = swap(y, "col", n_col, 1)
    end_bottom = along_z(bottom, out)
    own = share(sparse, xy, y)
    ones = share(one, end_top)
    far = joined(join_kernel, top, bottom)
    last = joined(pick_kernel, end_top, end_bottom, middle)
    pieces = [(2, far, share(far)), (0, sparse, own), (1, one, ones), (3, last, share(last))]
    return [sparse, x, y, xy], pieces


def gather(sparse, n_row, n_col):
    panels = [sparse]
    while len(panels) < n_col:
        panels += [swap(panel, "col", n_col, len(panels)) for panel in panels]
    blocks = [sparse] + [swap(sparse, "row", n_row, 2 * m) for m in range(1, n_row // 2)]
    return panels, [(m, own, swap(own, "row", n_row, 1)) for m, own in enumerate(blocks)]


def on_device(n_row, n_col, similarity, in_mask, out_mask):
    rows_loc, cols_loc = similarity.shape
    line = (n_row, n_col) == (8, 4)
    sparse, *halves, keep = masked(similarity, in_mask, out_mask, line)
    if line:
        panels, pieces = gather_line(sparse, halves, n_row, n_col)
    else:
        panels, pieces = gather(sparse, n_row, n_col)
    where = [m for m, _, _ in pieces]
    mine = [own for _, own, _ in pieces]
    theirs = [other for _, _, other in pieces]

    size = 2 * rows_loc * cols_loc
    operands = panels + mine[:-1] + theirs[:-1]
    acc, late_panel = pl.pallas_call(
        functools.partial(early_kernel, n_col, where[:-1], where[-1]),
        out_shape=(
            pltpu.VMEM((rows_loc, cols_loc), jnp.float32),
            pltpu.VMEM((rows_loc, cols_loc), jnp.bfloat16),
        ),
        in_specs=[VMEM] * len(operands),
        out_specs=(VMEM, VMEM),
        scratch_shapes=[pltpu.VMEM((n_col, rows_loc, cols_loc), jnp.bfloat16)],
        compiler_params=pltpu.CompilerParams(vmem_limit_bytes=(n_col + 8) * size),
    )(*map(resident, operands))
    inflated, sums = pl.pallas_call(
        late_kernel,
        out_shape=(
            pltpu.VMEM((rows_loc, cols_loc), jnp.float32),
            pltpu.VMEM((1, cols_loc), jnp.float32),
        ),
        in_specs=[SMEM] + [VMEM] * 4,
        out_specs=(VMEM, VMEM),
        compiler_params=pltpu.CompilerParams(vmem_limit_bytes=8 * size),
    )(keep, acc, late_panel, resident(mine[-1]), resident(theirs[-1]))

    step = 1
    while step < n_row:
        sums = sums + swap(sums, "row", n_row, step)
        step *= 2
    total = jnp.float32(rows_loc * n_row)
    return inflated * (total / sums)


def solution(mesh):
    in_specs = (P("row", "col"), P("row", "col"), P("row", "col"))
    out_specs = P("row", "col")
    body = functools.partial(on_device, mesh.shape["row"], mesh.shape["col"])
    return jax.shard_map(
        body, mesh=mesh, in_specs=in_specs, out_specs=out_specs, check_vma=False
    )
```
